256 devices in a mesh: tier: 8 (over y, core), mode: 32 (over x, z).
Axes of the slice: x: 4, y: 4, z: 8, core: 2. Of those that a mesh axis runs over, the one named last changes fastest.
Arguments:
- ados: float32 [8, 32, 2, 2, 9216], P('tier', 'mode'), may hold values from -6 to 6
- hamiltonian: float32 [96, 96], replicated, may hold values from -0.3125 to 0.3125
- couplings: float32 [16, 96], replicated, may hold values from -2.4 to 2.4
- rates: float32 [16], replicated, may hold values from 0.05 to 0.6
- strength: float32 [2, 16], replicated, may hold values from -1.8 to 1.8
- occupancy: int32 [8, 32, 2, 16], P('tier', 'mode'), may hold values from 0 to 8, as said below
- up_index: int32 [8, 32, 2, 16], P('tier', 'mode'), may hold values from 0 to 8, as said below
- down_index: int32 [8, 32, 2, 16], P('tier', 'mode'), may hold values from 0 to 8, as said below
Outputs:
- evolved: float32 [8, 32, 2, 2, 9216], P('tier', 'mode')
The draws below stay inside these ranges and needn't reach their ends.
Inputs may be any that keep to these rules, and one draw needn't show every extreme that they name: `occupancy`: each matrix is occupied in at most 8 quanta in all, summed over the 16 modes; higher tier bins hold matrices of higher tiers on average. For each mode, up_index and down_index describe the same pairs in the two directions: if the entry of matrix a for mode k in up_index names matrix b, then the entry of b for mode k in down_index names a, and the reverse; no matrix is named twice for one mode. The value 4 * 2 names no matrix, and no entry names a tier outside the hierarchy. `down_index`: see up_index.
All inputs are finite; a program needn't handle non-finite values.
Results may differ from the reference program's by a relative error of at most 0.00005.
Values sent between devices are 32-bit elements; how exact they have to be, the bound alone decides.
A program may use at most 64 MiB of HBM per device.

```python
import math
import jax
import jax.numpy as jnp
from jax import lax

D = 96
K = 16
DEPTH = 8
A_DEV = 2
TIER_BINS = 8
MODE_BINS = 32


def coupling_tables(key):
    base = jax.random.fold_in(key, 7)
    key_class, key_order, key_shift, key_turn = jax.random.split(base, 4)
    classes = jax.random.randint(key_class, (K, A_DEV), 0, 5)
    scores = jax.random.randint(key_order, (K, A_DEV), 0, 1 << 20) * A_DEV + jnp.arange(A_DEV)[None, :]
    order = jnp.argsort(scores, axis=1)
    inverse = jnp.argsort(order, axis=1)
    shifts = jax.random.randint(key_shift, (K, TIER_BINS, MODE_BINS), 0, A_DEV)
    turns = jax.random.randint(key_turn, (K, TIER_BINS, MODE_BINS), 0, A_DEV)
    return (classes, order, inverse, shifts, turns)


def draw_down_index(key, part):
    classes, order, inverse, shifts, turns = coupling_tables(key)
    tier_pos = jnp.arange(TIER_BINS)[:, None, None, None]
    mode_pos = jnp.arange(MODE_BINS)[None, :, None, None]
    slot_pos = jnp.arange(A_DEV)[None, None, :, None]
    mode_key = jnp.arange(K)[None, None, None, :]
    turn_now = turns[mode_key, tier_pos, mode_pos]
    rotated = order[mode_key, (slot_pos - turn_now) % A_DEV]
    kind = classes[mode_key, rotated]
    source_tier = tier_pos - kind % 2
    source_mode = (mode_pos - kind // 2) % MODE_BINS
    living = (kind < 4) & (source_tier >= 0)
    shift_now = shifts[mode_key, jnp.clip(source_tier, 0, TIER_BINS - 1), source_mode]
    source_slot = (rotated - shift_now) % A_DEV
    return jnp.where(living, kind * A_DEV + source_slot, 4 * A_DEV).astype(jnp.int32)


def draw_up_index(key, part):
    classes, order, inverse, shifts, turns = coupling_tables(key)
    tier_pos = jnp.arange(TIER_BINS)[:, None, None, None]
    mode_pos = jnp.arange(MODE_BINS)[None, :, None, None]
    slot_pos = jnp.arange(A_DEV)[None, None, :, None]
    mode_key = jnp.arange(K)[None, None, None, :]
    shift_now = shifts[mode_key, tier_pos, mode_pos]
    rotated = (slot_pos + shift_now) % A_DEV
    kind = classes[mode_key, rotated]
    target_tier = tier_pos + kind % 2
    target_mode = (mode_pos + kind // 2) % MODE_BINS
    living = (kind < 4) & (target_tier < TIER_BINS)
    turn_now = turns[mode_key, jnp.clip(target_tier, 0, TIER_BINS - 1), target_mode]
    target_slot = (inverse[mode_key, rotated] + turn_now) % A_DEV
    return jnp.where(living, kind * A_DEV + target_slot, 4 * A_DEV).astype(jnp.int32)


def draw_occupancy(key, part):
    base = jax.random.fold_in(key, 3)
    key_pick, key_live = jax.random.split(base, 2)
    picks = jax.random.randint(key_pick, (TIER_BINS, MODE_BINS, A_DEV, DEPTH), 0, K)
    tier_pos = jnp.arange(TIER_BINS)[:, None, None, None]
    slot_pos = jnp.arange(A_DEV)[None, None, :, None]
    chance = jax.random.randint(key_live, (TIER_BINS, MODE_BINS, A_DEV, DEPTH), 0, TIER_BINS + 1)
    living = chance <= tier_pos + 1
    filled = (tier_pos == TIER_BINS - 1) & (slot_pos == 0)
    filled = jnp.broadcast_to(filled, picks.shape)
    picks = jnp.where(filled, jnp.broadcast_to(picks[..., :1], picks.shape), picks)
    living = living | filled
    picks = jnp.where(living, picks, K)
    counts = jnp.sum((picks[..., None] == jnp.arange(K)[None, None, None, None, :]).astype(jnp.int32), axis=3)
    return counts.astype(jnp.int32)


def levels(own_key, extent, shards, low, high):
    loudness, own = 1.0, jax.random.fold_in(own_key, 6)
    for axis_at, blocks in shards:
        steps = jnp.exp(jax.random.uniform(jax.random.fold_in(own, axis_at), (blocks,), jnp.float32, low / len(shards), high / len(shards)))
        loudness = loudness * jnp.repeat(steps, extent[axis_at] // blocks).reshape([-1 if axis == axis_at else 1 for axis in range(len(extent))])
    return loudness


def scatter_about(stream_key, dims, deviation, limit, shards=(), kind=jnp.bfloat16):
    drawn = jax.random.normal(stream_key, dims, jnp.float32) * deviation
    if len(shards) > 0:
        drawn = levels(stream_key, dims, shards, -0.22, 0.18) * drawn
    return jnp.clip(drawn, min=-limit, max=limit).astype(kind)


def setup_inputs(seed: int = 0) -> dict:
    splits = jax.random.split(jax.random.key(seed), 9)
    return {
        "ados": scatter_about(splits[0], (TIER_BINS, MODE_BINS, A_DEV, 2, D * D), 1.0, 6.0, ((0, 8), (1, 32)), jnp.float32),
        "hamiltonian": scatter_about(splits[1], (D, D), (4 * D) ** -0.5, 0.3125, (), jnp.float32),
        "couplings": scatter_about(splits[2], (K, D), 0.4, 2.4, (), jnp.float32),
        "rates": jnp.clip(jnp.exp(jax.random.uniform(splits[3], (K,), jnp.float32, math.log(0.05), math.log(0.6))), 0.05, 0.6),
        "strength": scatter_about(splits[4], (2, K), 0.3, 1.8, (), jnp.float32),
        "occupancy": draw_occupancy(jax.random.fold_in(splits[8], 71), 0),
        "up_index": draw_up_index(jax.random.fold_in(splits[8], 71), 0),
        "down_index": draw_down_index(jax.random.fold_in(splits[8], 71), 0),
    }


TIME_STEP = 0.3


def fetch_rows(fields, index, direction):
    tier_count = fields.shape[0]
    mode_count = fields.shape[1]
    slot_count = fields.shape[2]
    tier_pos = jnp.arange(tier_count, dtype=jnp.int32)[:, None, None]
    mode_pos = jnp.arange(mode_count, dtype=jnp.int32)[None, :, None]
    block_pos = index // slot_count
    slot_pos = index % slot_count
    tier_step = block_pos % 2
    mode_step = block_pos // 2
    source_tier = tier_pos + direction * tier_step
    source_mode = (mode_pos + direction * mode_step) % mode_count
    living = (block_pos < 4) & (source_tier >= 0) & (source_tier < tier_count)
    picked = fields[jnp.clip(source_tier, 0, tier_count - 1), source_mode, slot_pos]
    return jnp.where(living[..., None, None], picked, jnp.zeros((), jnp.float32))


def derivative(fields, ham, gaps, sums, rates, strength, occupancy, up_index, down_index):
    tier_count, mode_count, slot_count = fields.shape[0], fields.shape[1], fields.shape[2]
    sys_width = ham.shape[0]
    square = (tier_count, mode_count, slot_count, sys_width, sys_width)
    flat_shape = (tier_count, mode_count, slot_count, sys_width * sys_width)
    real_part = fields[:, :, :, 0].reshape(square)
    imag_part = fields[:, :, :, 1].reshape(square)
    highest = lax.Precision.HIGHEST
    h_real = jnp.einsum("ij,tmajk->tmaik", ham, real_part, precision=highest)
    real_h = jnp.einsum("tmaij,jk->tmaik", real_part, ham, precision=highest)
    h_imag = jnp.einsum("ij,tmajk->tmaik", ham, imag_part, precision=highest)
    imag_h = jnp.einsum("tmaij,jk->tmaik", imag_part, ham, precision=highest)
    weights = occupancy.astype(jnp.float32)
    damping = jnp.einsum("tmak,k->tma", weights, rates, precision=highest)[..., None]
    d_real = (h_imag - imag_h).reshape(flat_shape) - damping * fields[:, :, :, 0]
    d_imag = (real_h - h_real).reshape(flat_shape) - damping * fields[:, :, :, 1]

    def add_mode(which, totals):
        acc_real, acc_imag = totals
        up_rows = fetch_rows(fields, lax.dynamic_index_in_dim(up_index, which, 3, False), 1)
        down_rows = fetch_rows(fields, lax.dynamic_index_in_dim(down_index, which, 3, False), -1)
        gap_row = lax.dynamic_index_in_dim(gaps, which, 0, False)
        plus_row = lax.dynamic_index_in_dim(sums, which, 0, False)
        level = lax.dynamic_index_in_dim(weights, which, 3, True)
        real_c = strength[0, which]
        imag_c = strength[1, which]
        acc_real = acc_real + gap_row * up_rows[:, :, :, 1] + level * (
            real_c * gap_row * down_rows[:, :, :, 1] + imag_c * plus_row * down_rows[:, :, :, 0])
        acc_imag = acc_imag - gap_row * up_rows[:, :, :, 0] - level * (
            real_c * gap_row * down_rows[:, :, :, 0] - imag_c * plus_row * down_rows[:, :, :, 1])
        return acc_real, acc_imag

    d_real, d_imag = lax.fori_loop(0, gaps.shape[0], add_mode, (d_real, d_imag))
    return jnp.stack([d_real, d_imag], axis=3)


def reference(ados, hamiltonian, couplings, rates, strength, occupancy, up_index, down_index):
    ham = 0.5 * (hamiltonian + hamiltonian.T)
    mode_total = couplings.shape[0]
    gaps = (couplings[:, :, None] - couplings[:, None, :]).reshape(mode_total, -1)
    sums = (couplings[:, :, None] + couplings[:, None, :]).reshape(mode_total, -1)

    def rhs(fields):
        return derivative(fields, ham, gaps, sums, rates, strength, occupancy, up_index, down_index)

    first = rhs(ados)
    second = rhs(ados + (TIME_STEP / 2) * first)
    third = rhs(ados + (TIME_STEP / 2) * second)
    fourth = rhs(ados + TIME_STEP * third)
    return ados + (TIME_STEP / 6) * (first + 2.0 * second + 2.0 * third + fourth)
```

```python
import jax
import jax.numpy as jnp
from jax import lax
from jax.experimental import pallas as pl
from jax.experimental.pallas import tpu as pltpu
from jax.sharding import PartitionSpec as P

TIME_STEP = 0.3
STAGES = 4
HIGHEST = lax.Precision.HIGHEST
MESH_ID = pl.DeviceIdType.MESH

LOWER_TIER, UPPER_TIER, LOWER_MODE, UPPER_MODE, LOWER_DIAG, UPPER_DIAG = range(6)
PIECES = 3
GROUPS = 24


def lane_index():
    return lax.broadcasted_iota(jnp.int32, (GROUPS, 128), 1)


def widen(row):
    lane = lax.broadcasted_iota(jnp.int32, row.shape, 1)
    by96, by64, by32 = (pltpu.roll(row, shift, 1) for shift in (96, 64, 32))
    return (
        jnp.where(lane < 96, row, by96),
        jnp.where(lane < 64, by96, by64),
        jnp.where(lane < 32, by64, by32),
    )


def unpack(pieces):
    lane = lane_index()
    first, second, third = pieces
    return jnp.concatenate(
        [
            first,
            jnp.where(lane < 32, pltpu.roll(first, 32, 1), pltpu.roll(second, 32, 1)),
            jnp.where(lane < 64, pltpu.roll(second, 64, 1), pltpu.roll(third, 64, 1)),
            pltpu.roll(third, 96, 1),
        ],
        axis=0,
    )


def pack(rows):
    lane = lane_index()
    part = [rows[GROUPS * p : GROUPS * (p + 1)] for p in range(4)]
    one96, two64 = pltpu.roll(part[1], 96, 1), pltpu.roll(part[2], 64, 1)
    return (
        jnp.where(lane < 96, part[0], one96),
        jnp.where(lane < 64, one96, two64),
        jnp.where(lane < 32, two64, pltpu.roll(part[3], 32, 1)),
    )


def kernel(
    a_ref, ham_ref, cpl_ref, rates_ref, strength_ref, occ_ref, up_ref, down_ref,
    out_ref,
    own, halo, acc, gap_up, gap_down, plus_down, ham_sq, ham_perm, tall, send_sem, recv_sem,
):
    tier, mode = lax.axis_index("tier"), lax.axis_index("mode")
    tiers, modes = lax.axis_size("tier"), lax.axis_size("mode")
    next_mode, prev_mode = lax.rem(mode + 1, modes), lax.rem(mode + modes - 1, modes)
    has_lower, has_upper = tier > 0, tier < tiers - 1

    barrier = pltpu.get_barrier_semaphore()

    def greet(device):
        pl.semaphore_signal(barrier, inc=1, device_id=device, device_id_type=MESH_ID)

    greet((tier, next_mode))
    greet((tier, prev_mode))

    @pl.when(has_upper)
    def _():
        greet((tier + 1, mode))

    @pl.when(has_lower)
    def _():
        greet((tier - 1, mode))

    for s in range(2):
        for ri in range(2):
            for u in range(PIECES):
                own[0, u, 2 * s + ri] = a_ref[s, pl.ds(2 * u + ri, GROUPS, stride=6), :]

    blank = jnp.zeros((4, GROUPS, 128), jnp.float32)

    @pl.when(jnp.logical_not(has_lower))
    def _():
        for n in range(STAGES):
            for u in range(PIECES):
                halo[n, LOWER_TIER, u] = blank
                halo[n, LOWER_DIAG, u] = blank

    @pl.when(jnp.logical_not(has_upper))
    def _():
        for n in range(STAGES):
            for u in range(PIECES):
                halo[n, UPPER_TIER, u] = blank
                halo[n, UPPER_DIAG, u] = blank

    @pl.when(jnp.logical_and(has_upper, has_lower))
    def _():
        pl.semaphore_wait(barrier, 4)

    @pl.when(jnp.logical_not(jnp.logical_and(has_upper, has_lower)))
    def _():
        pl.semaphore_wait(barrier, 3)

    def copy(n, slot, u, src, device):
        return pltpu.make_async_remote_copy(
            src_ref=src,
            dst_ref=halo.at[n, slot, u],
            send_sem=send_sem.at[n, slot, u],
            recv_sem=recv_sem.at[n, slot, u],
            device_id=device,
            device_id_type=MESH_ID,
        )

    def copies(n, slot, u):
        source = {
            LOWER_DIAG: halo.at[n, LOWER_MODE, u],
            UPPER_DIAG: halo.at[n, UPPER_MODE, u],
        }.get(slot, own.at[n, u])
        device = {
            LOWER_TIER: (tier + 1, mode),
            LOWER_DIAG: (tier + 1, mode),
            UPPER_TIER: (tier - 1, mode),
            UPPER_DIAG: (tier - 1, mode),
            LOWER_MODE: (tier, next_mode),
            UPPER_MODE: (tier, prev_mode),
        }[slot]
        return copy(n, slot, u, source, device)

    sends_if = {
        LOWER_TIER: has_upper, LOWER_DIAG: has_upper,
        UPPER_TIER: has_lower, UPPER_DIAG: has_lower,
        LOWER_MODE: None, UPPER_MODE: None,
    }
    comes_if = {
        LOWER_TIER: has_lower, LOWER_DIAG: has_lower,
        UPPER_TIER: has_upper, UPPER_DIAG: has_upper,
        LOWER_MODE: None, UPPER_MODE: None,
    }

    def when(condition, act):
        if condition is None:
            act()
        else:
            pl.when(condition)(act)

    def start(n, slot, u):
        when(sends_if[slot], lambda: copies(n, slot, u).start())

    def arrive(n, slot, u):
        when(comes_if[slot], lambda: copies(n, slot, u).wait_recv())

    def send_own(n, u):
        for slot in (LOWER_MODE, UPPER_MODE, LOWER_TIER, UPPER_TIER):
            start(n, slot, u)

    for u in range(PIECES):
        send_own(0, u)

    raw = ham_ref[...]
    ham_sq[...] = jnp.zeros((128, 128), jnp.float32)
    ham_sq[:96, :96] = 0.5 * (raw + raw.T)
    rows = jnp.concatenate([ham_sq[pl.ds(p, GROUPS, stride=4), :] for p in range(4)], axis=0)
    tall[...] = jnp.concatenate([rows, jnp.zeros((32, 128), jnp.float32)], axis=0).T
    ham_perm[...] = jnp.concatenate([tall[pl.ds(p, GROUPS, stride=4), :] for p in range(4)], axis=0)

    level = occ_ref[...].astype(jnp.float32)
    named = lax.broadcasted_iota(jnp.int32, (8, 16), 0)
    ups, down_re, down_im = [], [], []
    for s in range(2):
        up_mask = (up_ref[s : s + 1, :] == named).astype(jnp.float32)
        down_mask = (down_ref[s : s + 1, :] == named).astype(jnp.float32) * level[s : s + 1, :]
        ups.append(up_mask)
        down_re.append(down_mask * strength_ref[0:1, :])
        down_im.append(down_mask * strength_ref[1:2, :])
    own_rows = lax.broadcasted_iota(jnp.int32, (8, 16), 0) < 2
    down_re = [d + jnp.where(own_rows, v, 0.0) for d, v in zip(down_re, ups)]
    mix = jnp.concatenate(ups + down_re + down_im, axis=0)
    cpl = cpl_ref[...]
    wide_cpl = jnp.concatenate([cpl, jnp.zeros((16, 32), jnp.float32)], axis=1)
    by_lane = jnp.dot(mix, wide_cpl, precision=HIGHEST, preferred_element_type=jnp.float32)
    flat = lax.dot_general(
        wide_cpl, mix, (((0,), (1,)), ((), ())), precision=HIGHEST, preferred_element_type=jnp.float32
    )
    tall[:, :48] = flat
    columns = [tall[pl.ds(p, GROUPS, stride=4), :] for p in range(4)]
    lane = lane_index()
    lanes_wide = widen(by_lane)
    damping = jnp.sum(level * rates_ref[...], axis=1, keepdims=True)
    for e in range(48):
        kind, s, source = e // 16, e // 8 % 2, e % 8
        if kind == 0 and source < 2:
            continue
        spread = [jnp.broadcast_to(columns[p][:, e : e + 1], (GROUPS, 128)) for p in range(4)]
        for u in range(PIECES):
            along_rows = jnp.where(lane < (96, 64, 32)[u], spread[u], spread[u + 1])
            along_lanes = lanes_wide[u][e : e + 1, :]
            if kind == 0:
                gap_up[8 * s + source, u] = along_rows - along_lanes
            elif kind == 1:
                gap_down[8 * s + source, u] = along_rows - along_lanes
            else:
                plus = along_rows + along_lanes
                if source == s:
                    plus = plus - damping[s : s + 1, :]
                plus_down[8 * s + source, u] = plus

    def add_up(sums, src, block, u):
        for j in range(2):
            real, imag = src[2 * j], src[2 * j + 1]
            for s in range(2):
                gap = gap_up[8 * s + 2 * block + j, u]
                sums[2 * s] = sums[2 * s] + gap * imag
                sums[2 * s + 1] = sums[2 * s + 1] - gap * real

    def add_down(sums, src, block, u):
        for j in range(2):
            real, imag = src[2 * j], src[2 * j + 1]
            for s in range(2):
                gap, plus = gap_down[8 * s + 2 * block + j, u], plus_down[8 * s + 2 * block + j, u]
                sums[2 * s] = sums[2 * s] + gap * imag + plus * real
                sums[2 * s + 1] = sums[2 * s + 1] + plus * imag - gap * real

    for n in range(STAGES):
        whole = [unpack([own[n, u, c] for u in range(PIECES)]) for c in range(4)]
        right = jnp.dot(
            jnp.concatenate(whole, axis=0), ham_sq[...], precision=HIGHEST, preferred_element_type=jnp.float32
        )
        left = jnp.dot(
            ham_perm[:, :96], jnp.concatenate(whole, axis=1), precision=HIGHEST, preferred_element_type=jnp.float32
        )
        moved = [pack(left[:, 128 * c : 128 * (c + 1)] - right[96 * c : 96 * (c + 1)]) for c in range(4)]
        for u in range(PIECES):
            sums = [moved[1][u], -moved[0][u], moved[3][u], -moved[2][u]]
            add_down(sums, own.at[n, u], 0, u)
            for c in range(4):
                acc[u, c] = sums[c]

        for u in range(PIECES):
            arrive(n, LOWER_MODE, u)
            start(n, LOWER_DIAG, u)
            arrive(n, UPPER_MODE, u)
            start(n, UPPER_DIAG, u)
            arrive(n, LOWER_TIER, u)
            arrive(n, UPPER_TIER, u)
            sums = [acc[u, c] for c in range(4)]
            add_down(sums, halo.at[n, LOWER_MODE, u], 2, u)
            add_up(sums, halo.at[n, UPPER_MODE, u], 2, u)
            add_down(sums, halo.at[n, LOWER_TIER, u], 1, u)
            add_up(sums, halo.at[n, UPPER_TIER, u], 1, u)
            for c in range(4):
                acc[u, c] = sums[c]

        for u in range(PIECES):
            arrive(n, LOWER_DIAG, u)
            arrive(n, UPPER_DIAG, u)
            sums = [acc[u, c] for c in range(4)]
            add_down(sums, halo.at[n, LOWER_DIAG, u], 3, u)
            add_up(sums, halo.at[n, UPPER_DIAG, u], 3, u)
            for c in range(4):
                term = (TIME_STEP / (n + 1)) * sums[c]
                if n < STAGES - 1:
                    own[n + 1, u, c] = term
                else:
                    total = term
                    for back in range(STAGES - 1, -1, -1):
                        total = total + own[back, u, c]
                    out_ref[c // 2, pl.ds(2 * u + c % 2, GROUPS, stride=6), :] = total
            if n < STAGES - 1:
                send_own(n + 1, u)

    for n in range(STAGES):
        for u in range(PIECES):
            for slot in range(6):
                when(sends_if[slot], lambda n=n, slot=slot, u=u: copies(n, slot, u).wait_send())


def shards(ados, hamiltonian, couplings, rates, strength, occupancy, up_index, down_index):
    rows = ados.reshape(2, 2, 72, 128).transpose(0, 2, 1, 3).reshape(2, 144, 128)
    vmem = pl.BlockSpec(memory_space=pltpu.VMEM)
    done = pl.pallas_call(
        kernel,
        out_shape=jax.ShapeDtypeStruct((2, 144, 128), jnp.float32),
        in_specs=[vmem] * 8,
        out_specs=vmem,
        scratch_shapes=[
            pltpu.VMEM((STAGES, PIECES, 4, GROUPS, 128), jnp.float32),
            pltpu.VMEM((STAGES, 6, PIECES, 4, GROUPS, 128), jnp.float32),
            pltpu.VMEM((PIECES, 4, GROUPS, 128), jnp.float32),
            pltpu.VMEM((16, PIECES, GROUPS, 128), jnp.float32),
            pltpu.VMEM((16, PIECES, GROUPS, 128), jnp.float32),
            pltpu.VMEM((16, PIECES, GROUPS, 128), jnp.float32),
            pltpu.VMEM((128, 128), jnp.float32),
            pltpu.VMEM((96, 128), jnp.float32),
            pltpu.VMEM((128, 128), jnp.float32),
            pltpu.SemaphoreType.DMA((STAGES, 6, PIECES)),
            pltpu.SemaphoreType.DMA((STAGES, 6, PIECES)),
        ],
        compiler_params=pltpu.CompilerParams(collective_id=0, has_side_effects=True),
    )(
        rows, hamiltonian, couplings, rates.reshape(1, -1), strength,
        occupancy.reshape(2, -1), up_index.reshape(2, -1), down_index.reshape(2, -1),
    )
    return done.reshape(2, 72, 2, 128).transpose(0, 2, 1, 3).reshape(ados.shape)


def solution(mesh):
    split = P("tier", "mode", None, None)
    in_specs = (P("tier", "mode", None, None, None), P(), P(), P(), P(), split, split, split)
    out_specs = P("tier", "mode", None, None, None)
    return jax.shard_map(shards, mesh=mesh, in_specs=in_specs, out_specs=out_specs, check_vma=False)
```

```python
import jax
import jax.numpy as jnp
from jax import lax
from jax.experimental import pallas as pl
from jax.experimental.pallas import tpu as pltpu
from jax.sharding import PartitionSpec as P

TIME_STEP = 0.3
STAGES = 4
HIGHEST = lax.Precision.HIGHEST
MESH_ID = pl.DeviceIdType.MESH

LOWER_TIER, UPPER_TIER, LOWER_MODE, UPPER_MODE, LOWER_DIAG, UPPER_DIAG = range(6)
PARTS = 3
SLABS = 9
GROUPS = 24
CUTS = (0, 1, 3, 5, 7, 9)
PIECES = len(CUTS) - 1
LAG = 1


def lane_index():
    return lax.broadcasted_iota(jnp.int32, (GROUPS, 128), 1)


def widen(row):
    lane = lax.broadcasted_iota(jnp.int32, row.shape, 1)
    by96, by64, by32 = (pltpu.roll(row, shift, 1) for shift in (96, 64, 32))
    return (
        jnp.where(lane < 96, row, by96),
        jnp.where(lane < 64, by96, by64),
        jnp.where(lane < 32, by64, by32),
    )


def unpack(parts):
    lane = lane_index()
    first, second, third = parts
    return jnp.concatenate(
        [
            first,
            jnp.where(lane < 32, pltpu.roll(first, 32, 1), pltpu.roll(second, 32, 1)),
            jnp.where(lane < 64, pltpu.roll(second, 64, 1), pltpu.roll(third, 64, 1)),
            pltpu.roll(third, 96, 1),
        ],
        axis=0,
    )


def pack(rows):
    lane = lane_index()
    part = [rows[GROUPS * p : GROUPS * (p + 1)] for p in range(4)]
    one96, two64 = pltpu.roll(part[1], 96, 1), pltpu.roll(part[2], 64, 1)
    return (
        jnp.where(lane < 96, part[0], one96),
        jnp.where(lane < 64, one96, two64),
        jnp.where(lane < 32, two64, pltpu.roll(part[3], 32, 1)),
    )


def kernel(
    a_hbm, ham_hbm, cpl_hbm, rates_hbm, strength_hbm, occ_hbm, up_hbm, down_hbm,
    out_ref,
    a_ref, ham_ref, cpl_ref, rates_ref, strength_ref, occ_ref, up_ref, down_ref, load_sem,
    own, halo, acc, gap_up, gap_down, plus_down, ham_sq, ham_perm, tall, send_sem, recv_sem,
):
    tier, mode = lax.axis_index("tier"), lax.axis_index("mode")
    tiers, modes = lax.axis_size("tier"), lax.axis_size("mode")
    next_mode, prev_mode = lax.rem(mode + 1, modes), lax.rem(mode + modes - 1, modes)
    odd = lax.rem(tier, 2)
    partner = tier + 1 - 2 * odd
    across = lax.rem(tier + 2 * odd + tiers - 1, tiers)
    across_mode = lax.rem(mode + 2 * odd + modes - 1, modes)
    has_across = jnp.logical_and(tier > 0, tier < tiers - 1)

    barrier = pltpu.get_barrier_semaphore()

    def greet(device):
        pl.semaphore_signal(barrier, inc=1, device_id=device, device_id_type=MESH_ID)

    greet((tier, next_mode))
    greet((tier, prev_mode))
    greet((partner, mode))

    @pl.when(has_across)
    def _():
        greet((across, mode))
        greet((across, across_mode))

    loads = [
        pltpu.make_async_copy(src, dst, load_sem.at[i])
        for i, (src, dst) in enumerate(
            zip(
                (a_hbm, ham_hbm, cpl_hbm, rates_hbm, strength_hbm, occ_hbm, up_hbm, down_hbm),
                (a_ref, ham_ref, cpl_ref, rates_ref, strength_ref, occ_ref, up_ref, down_ref),
            )
        )
    ]
    for load in loads:
        load.start()
    loads[0].wait()

    def place(k):
        return k % PARTS, 8 * (k // PARTS)

    for k in range(SLABS):
        u, q = place(k)
        for c in range(4):
            own[0, k, c] = a_ref[c // 2, pl.ds(6 * q + 2 * u + c % 2, 8, stride=6), :]

    @pl.when(has_across)
    def _():
        pl.semaphore_wait(barrier, 5)

    @pl.when(jnp.logical_not(has_across))
    def _():
        pl.semaphore_wait(barrier, 3)

    def copy(n, slot, p, src, device):
        span = pl.ds(CUTS[p], CUTS[p + 1] - CUTS[p])
        return pltpu.make_async_remote_copy(
            src_ref=src.at[span],
            dst_ref=halo.at[n, slot, span],
            send_sem=send_sem.at[n, slot],
            recv_sem=recv_sem.at[n, slot, p],
            device_id=device,
            device_id_type=MESH_ID,
        )

    def arrive(n, slot, p):
        copy(n, slot, p, own.at[n], (partner, mode)).wait_recv()

    def send_own(n, p):
        mine = own.at[n]
        copy(n, LOWER_MODE, p, mine, (tier, next_mode)).start()
        copy(n, UPPER_MODE, p, mine, (tier, prev_mode)).start()

        @pl.when(has_across)
        def _():
            copy(n, UPPER_DIAG - odd, p, mine, (across, across_mode)).start()
            copy(n, UPPER_TIER - odd, p, mine, (across, mode)).start()

        copy(n, LOWER_TIER + odd, p, mine, (partner, mode)).start()

    def relay(n, p):
        copy(n, LOWER_DIAG + odd, p, halo.at[n, LOWER_MODE + odd], (partner, mode)).start()

    for p in range(PIECES):
        send_own(0, p)

    blank = jnp.zeros((4, 8, 128), jnp.float32)

    @pl.when(jnp.logical_not(has_across))
    def _():
        for n in range(STAGES):
            for k in range(SLABS):
                halo[n, LOWER_TIER + odd, k] = blank
                halo[n, LOWER_DIAG + odd, k] = blank

    for load in loads[1:]:
        load.wait()

    raw = ham_ref[...]
    ham_sq[...] = jnp.zeros((128, 128), jnp.float32)
    ham_sq[:96, :96] = 0.5 * (raw + raw.T)
    rows = jnp.concatenate([ham_sq[pl.ds(p, GROUPS, stride=4), :] for p in range(4)], axis=0)
    tall[...] = jnp.concatenate([rows, jnp.zeros((32, 128), jnp.float32)], axis=0).T
    ham_perm[...] = jnp.concatenate([tall[pl.ds(p, GROUPS, stride=4), :] for p in range(4)], axis=0)

    level = occ_ref[...].astype(jnp.float32)
    named = lax.broadcasted_iota(jnp.int32, (8, 16), 0)
    ups, down_re, down_im = [], [], []
    for s in range(2):
        up_mask = (up_ref[s : s + 1, :] == named).astype(jnp.float32)
        down_mask = (down_ref[s : s + 1, :] == named).astype(jnp.float32) * level[s : s + 1, :]
        ups.append(up_mask)
        down_re.append(down_mask * strength_ref[0:1, :])
        down_im.append(down_mask * strength_ref[1:2, :])
    own_rows = lax.broadcasted_iota(jnp.int32, (8, 16), 0) < 2
    down_re = [d + jnp.where(own_rows, v, 0.0) for d, v in zip(down_re, ups)]
    mix = jnp.concatenate(ups + down_re + down_im, axis=0)
    cpl = cpl_ref[...]
    wide_cpl = jnp.concatenate([cpl, jnp.zeros((16, 32), jnp.float32)], axis=1)
    by_lane = jnp.dot(mix, wide_cpl, precision=HIGHEST, preferred_element_type=jnp.float32)
    flat = lax.dot_general(
        wide_cpl, mix, (((0,), (1,)), ((), ())), precision=HIGHEST, preferred_element_type=jnp.float32
    )
    tall[:, :48] = flat
    columns = [tall[pl.ds(p, GROUPS, stride=4), :] for p in range(4)]
    lane = lane_index()
    lanes_wide = widen(by_lane)
    damping = jnp.sum(level * rates_ref[...], axis=1, keepdims=True)
    for e in range(48):
        kind, s, source = e // 16, e // 8 % 2, e % 8
        if kind == 0 and source < 2:
            continue
        spread = [jnp.broadcast_to(columns[p][:, e : e + 1], (GROUPS, 128)) for p in range(4)]
        for u in range(PARTS):
            along_rows = jnp.where(lane < (96, 64, 32)[u], spread[u], spread[u + 1])
            along_lanes = lanes_wide[u][e : e + 1, :]
            if kind == 0:
                gap_up[8 * s + source, u] = along_rows - along_lanes
            elif kind == 1:
                gap_down[8 * s + source, u] = along_rows - along_lanes
            else:
                plus = along_rows + along_lanes
                if source == s:
                    plus = plus - damping[s : s + 1, :]
                plus_down[8 * s + source, u] = plus

    def add_up(sums, src, block, k):
        u, q = place(k)
        for j in range(2):
            real, imag = src[2 * j], src[2 * j + 1]
            for s in range(2):
                gap = gap_up[8 * s + 2 * block + j, u, q : q + 8]
                sums[2 * s] = sums[2 * s] + gap * imag
                sums[2 * s + 1] = sums[2 * s + 1] - gap * real

    def add_down(sums, src, block, k):
        u, q = place(k)
        for j in range(2):
            real, imag = src[2 * j], src[2 * j + 1]
            for s in range(2):
                at = 8 * s + 2 * block + j
                gap, plus = gap_down[at, u, q : q + 8], plus_down[at, u, q : q + 8]
                sums[2 * s] = sums[2 * s] + gap * imag + plus * real
                sums[2 * s + 1] = sums[2 * s + 1] + plus * imag - gap * real

    def local(n):
        whole = [
            unpack([jnp.concatenate([own[n, PARTS * o + u, c] for o in range(3)], axis=0) for u in range(PARTS)])
            for c in range(4)
        ]
        right = jnp.dot(
            jnp.concatenate(whole, axis=0), ham_sq[...], precision=HIGHEST, preferred_element_type=jnp.float32
        )
        left = jnp.dot(
            ham_perm[:, :96], jnp.concatenate(whole, axis=1), precision=HIGHEST, preferred_element_type=jnp.float32
        )
        moved = [pack(left[:, 128 * c : 128 * (c + 1)] - right[96 * c : 96 * (c + 1)]) for c in range(4)]
        for k in range(SLABS):
            u, q = place(k)
            here = [part[u][q : q + 8] for part in moved]
            sums = [here[1], -here[0], here[3], -here[2]]
            add_down(sums, own.at[n, k], 0, k)
            for c in range(4):
                acc[k, c] = sums[c]

    def gather(n, p):
        arrive(n, LOWER_MODE + odd, p)
        relay(n, p)
        arrive(n, UPPER_MODE - odd, p)
        arrive(n, UPPER_TIER - odd, p)

        @pl.when(has_across)
        def _():
            arrive(n, LOWER_TIER + odd, p)

        for k in range(CUTS[p], CUTS[p + 1]):
            sums = [acc[k, c] for c in range(4)]
            add_down(sums, halo.at[n, LOWER_MODE, k], 2, k)
            add_up(sums, halo.at[n, UPPER_MODE, k], 2, k)
            add_down(sums, halo.at[n, LOWER_TIER, k], 1, k)
            add_up(sums, halo.at[n, UPPER_TIER, k], 1, k)
            for c in range(4):
                acc[k, c] = sums[c]

    def finish(n, p):
        arrive(n, UPPER_DIAG - odd, p)

        @pl.when(has_across)
        def _():
            arrive(n, LOWER_DIAG + odd, p)

        for k in range(CUTS[p], CUTS[p + 1]):
            u, q = place(k)
            sums = [acc[k, c] for c in range(4)]
            add_down(sums, halo.at[n, LOWER_DIAG, k], 3, k)
            add_up(sums, halo.at[n, UPPER_DIAG, k], 3, k)
            for c in range(4):
                term = (TIME_STEP / (n + 1)) * sums[c]
                if n < STAGES - 1:
                    own[n + 1, k, c] = term
                else:
                    total = term
                    for back in range(STAGES - 1, -1, -1):
                        total = total + own[back, k, c]
                    out_ref[c // 2, pl.ds(6 * q + 2 * u + c % 2, 8, stride=6), :] = total
        if n < STAGES - 1:
            send_own(n + 1, p)

    for n in range(STAGES):
        local(n)
        for p in range(PIECES + LAG):
            if p < PIECES:
                gather(n, p)
            if p >= LAG:
                finish(n, p - LAG)

    def sent(n, slot):
        pltpu.make_async_remote_copy(
            src_ref=own.at[n],
            dst_ref=halo.at[n, slot],
            send_sem=send_sem.at[n, slot],
            recv_sem=recv_sem.at[n, slot, 0],
            device_id=(partner, mode),
            device_id_type=MESH_ID,
        ).wait_send()

    for n in range(STAGES):
        sent(n, LOWER_MODE)
        sent(n, UPPER_MODE)
        sent(n, LOWER_TIER + odd)
        sent(n, LOWER_DIAG + odd)

        @pl.when(has_across)
        def _():
            sent(n, UPPER_TIER - odd)
            sent(n, UPPER_DIAG - odd)


def shards(ados, hamiltonian, couplings, rates, strength, occupancy, up_index, down_index):
    rows = ados.reshape(2, 2, 72, 128).transpose(0, 2, 1, 3).reshape(2, 144, 128)
    operands = (
        rows, hamiltonian, couplings, rates.reshape(1, -1), strength,
        occupancy.reshape(2, -1), up_index.reshape(2, -1), down_index.reshape(2, -1),
    )
    real = jnp.float32
    done = pl.pallas_call(
        kernel,
        out_shape=jax.ShapeDtypeStruct((2, 144, 128), real),
        in_specs=[pl.BlockSpec(memory_space=pl.ANY)] * 8,
        out_specs=pl.BlockSpec(memory_space=pltpu.VMEM),
        scratch_shapes=[pltpu.VMEM(x.shape, x.dtype) for x in operands] + [
            pltpu.SemaphoreType.DMA((8,)),
            pltpu.VMEM((STAGES, SLABS, 4, 8, 128), real),
            pltpu.VMEM((STAGES, 6, SLABS, 4, 8, 128), real),
            pltpu.VMEM((SLABS, 4, 8, 128), real),
            pltpu.VMEM((16, PARTS, GROUPS, 128), real),
            pltpu.VMEM((16, PARTS, GROUPS, 128), real),
            pltpu.VMEM((16, PARTS, GROUPS, 128), real),
            pltpu.VMEM((128, 128), real),
            pltpu.VMEM((96, 128), real),
            pltpu.VMEM((128, 128), real),
            pltpu.SemaphoreType.DMA((STAGES, 6)),
            pltpu.SemaphoreType.DMA((STAGES, 6, PIECES)),
        ],
        compiler_params=pltpu.CompilerParams(collective_id=0, has_side_effects=True),
    )(*operands)
    return done.reshape(2, 72, 2, 128).transpose(0, 2, 1, 3).reshape(ados.shape)


def solution(mesh):
    split = P("tier", "mode", None, None)
    in_specs = (P("tier", "mode", None, None, None), P(), P(), P(), P(), split, split, split)
    out_specs = P("tier", "mode", None, None, None)
    return jax.shard_map(shards, mesh=mesh, in_specs=in_specs, out_specs=out_specs, check_vma=False)
```

```python
import jax
import jax.numpy as jnp
from jax import lax
from jax.experimental import pallas as pl
from jax.experimental.pallas import tpu as pltpu
from jax.sharding import PartitionSpec as P

TIME_STEP = 0.3
STAGES = 4
HIGHEST = lax.Precision.HIGHEST
MESH_ID = pl.DeviceIdType.MESH

LOWER_TIER, UPPER_TIER, LOWER_MODE, UPPER_MODE, LOWER_DIAG, UPPER_DIAG = range(6)
PARTS = 3
SLABS = 9
GROUPS = 24
CUTS = (0, 1, 3, 5, 7, 9)
PIECES = len(CUTS) - 1
LAG = 1


def lane_index():
    return lax.broadcasted_iota(jnp.int32, (GROUPS, 128), 1)


def widen(row):
    lane = lax.broadcasted_iota(jnp.int32, row.shape, 1)
    by96, by64, by32 = (pltpu.roll(row, shift, 1) for shift in (96, 64, 32))
    return (
        jnp.where(lane < 96, row, by96),
        jnp.where(lane < 64, by96, by64),
        jnp.where(lane < 32, by64, by32),
    )


def unpack(parts):
    lane = lane_index()
    first, second, third = parts
    return jnp.concatenate(
        [
            first,
            jnp.where(lane < 32, pltpu.roll(first, 32, 1), pltpu.roll(second, 32, 1)),
            jnp.where(lane < 64, pltpu.roll(second, 64, 1), pltpu.roll(third, 64, 1)),
            pltpu.roll(third, 96, 1),
        ],
        axis=0,
    )


def pack(rows):
    lane = lane_index()
    part = [rows[GROUPS * p : GROUPS * (p + 1)] for p in range(4)]
    one96, two64 = pltpu.roll(part[1], 96, 1), pltpu.roll(part[2], 64, 1)
    return (
        jnp.where(lane < 96, part[0], one96),
        jnp.where(lane < 64, one96, two64),
        jnp.where(lane < 32, two64, pltpu.roll(part[3], 32, 1)),
    )


def kernel(
    a_hbm, ham_hbm, cpl_hbm, rates_hbm, strength_hbm, occ_hbm, up_hbm, down_hbm,
    out_ref,
    a_ref, ham_ref, cpl_ref, rates_ref, strength_ref, occ_ref, up_ref, down_ref, load_sem,
    own, halo, acc, gap_up, gap_down, plus_down, ham_sq, ham_perm, tall, send_sem, recv_sem,
):
    tier, mode = lax.axis_index("tier"), lax.axis_index("mode")
    tiers, modes = lax.axis_size("tier"), lax.axis_size("mode")
    next_mode, prev_mode = lax.rem(mode + 1, modes), lax.rem(mode + modes - 1, modes)
    odd = lax.rem(tier, 2)
    partner = tier + 1 - 2 * odd
    across = lax.rem(tier + 2 * odd + tiers - 1, tiers)
    across_mode = lax.rem(mode + 2 * odd + modes - 1, modes)
    has_across = jnp.logical_and(tier > 0, tier < tiers - 1)

    barrier = pltpu.get_barrier_semaphore()

    def greet(device):
        pl.semaphore_signal(barrier, inc=1, device_id=device, device_id_type=MESH_ID)

    greet((tier, next_mode))
    greet((tier, prev_mode))
    greet((partner, mode))

    @pl.when(has_across)
    def _():
        greet((across, mode))
        greet((across, across_mode))

    loads = [
        pltpu.make_async_copy(src, dst, load_sem.at[i])
        for i, (src, dst) in enumerate(
            zip(
                (a_hbm, ham_hbm, cpl_hbm, rates_hbm, strength_hbm, occ_hbm, up_hbm, down_hbm),
                (a_ref, ham_ref, cpl_ref, rates_ref, strength_ref, occ_ref, up_ref, down_ref),
            )
        )
    ]
    for load in loads:
        load.start()
    loads[0].wait()

    def place(k):
        return k % PARTS, 8 * (k // PARTS)

    for k in range(SLABS):
        u, q = place(k)
        for c in range(4):
            own[0, k, c] = a_ref[c // 2, pl.ds(6 * q + 2 * u + c % 2, 8, stride=6), :]

    @pl.when(has_across)
    def _():
        pl.semaphore_wait(barrier, 5)

    @pl.when(jnp.logical_not(has_across))
    def _():
        pl.semaphore_wait(barrier, 3)

    def copy(n, slot, p, src, device):
        span = pl.ds(CUTS[p], CUTS[p + 1] - CUTS[p])
        return pltpu.make_async_remote_copy(
            src_ref=src.at[span],
            dst_ref=halo.at[n, slot, span],
            send_sem=send_sem.at[n, slot],
            recv_sem=recv_sem.at[n, slot, p],
            device_id=device,
            device_id_type=MESH_ID,
        )

    def arrive(n, slot, p):
        copy(n, slot, p, own.at[n], (partner, mode)).wait_recv()

    def send_own(n, p):
        mine = own.at[n]
        copy(n, LOWER_MODE, p, mine, (tier, next_mode)).start()
        copy(n, UPPER_MODE, p, mine, (tier, prev_mode)).start()

        @pl.when(has_across)
        def _():
            copy(n, UPPER_DIAG - odd, p, mine, (across, across_mode)).start()
            copy(n, UPPER_TIER - odd, p, mine, (across, mode)).start()

        copy(n, LOWER_TIER + odd, p, mine, (partner, mode)).start()

    def relay(n, p):
        copy(n, LOWER_DIAG + odd, p, halo.at[n, LOWER_MODE + odd], (partner, mode)).start()

    for p in range(PIECES):
        send_own(0, p)

    blank = jnp.zeros((4, 8, 128), jnp.float32)

    @pl.when(jnp.logical_not(has_across))
    def _():
        for n in range(STAGES):
            for k in range(SLABS):
                halo[n, LOWER_TIER + odd, k] = blank
                halo[n, LOWER_DIAG + odd, k] = blank

    for load in loads[1:]:
        load.wait()

    raw = ham_ref[...]
    ham_sq[...] = jnp.zeros((128, 128), jnp.float32)
    ham_sq[:96, :96] = 0.5 * (raw + raw.T)
    rows = jnp.concatenate([ham_sq[pl.ds(p, GROUPS, stride=4), :] for p in range(4)], axis=0)
    tall[...] = jnp.concatenate([rows, jnp.zeros((32, 128), jnp.float32)], axis=0).T
    ham_perm[...] = jnp.concatenate([tall[pl.ds(p, GROUPS, stride=4), :] for p in range(4)], axis=0)

    level = occ_ref[...].astype(jnp.float32)
    named = lax.broadcasted_iota(jnp.int32, (8, 16), 0)
    ups, down_re, down_im = [], [], []
    for s in range(2):
        up_mask = (up_ref[s : s + 1, :] == named).astype(jnp.float32)
        down_mask = (down_ref[s : s + 1, :] == named).astype(jnp.float32) * level[s : s + 1, :]
        ups.append(up_mask)
        down_re.append(down_mask * strength_ref[0:1, :])
        down_im.append(down_mask * strength_ref[1:2, :])
    own_rows = lax.broadcasted_iota(jnp.int32, (8, 16), 0) < 2
    down_re = [d + jnp.where(own_rows, v, 0.0) for d, v in zip(down_re, ups)]
    mix = jnp.concatenate(ups + down_re + down_im, axis=0)
    cpl = cpl_ref[...]
    wide_cpl = jnp.concatenate([cpl, jnp.zeros((16, 32), jnp.float32)], axis=1)
    by_lane = jnp.dot(mix, wide_cpl, precision=HIGHEST, preferred_element_type=jnp.float32)
    flat = lax.dot_general(
        wide_cpl, mix, (((0,), (1,)), ((), ())), precision=HIGHEST, preferred_element_type=jnp.float32
    )
    tall[:, :48] = flat
    columns = [tall[pl.ds(p, GROUPS, stride=4), :] for p in range(4)]
    lane = lane_index()
    lanes_wide = widen(by_lane)
    damping = jnp.sum(level * rates_ref[...], axis=1, keepdims=True)
    for e in range(48):
        kind, s, source = e // 16, e // 8 % 2, e % 8
        if kind == 0 and source < 2:
            continue
        spread = [jnp.broadcast_to(columns[p][:, e : e + 1], (GROUPS, 128)) for p in range(4)]
        for u in range(PARTS):
            along_rows = jnp.where(lane < (96, 64, 32)[u], spread[u], spread[u + 1])
            along_lanes = lanes_wide[u][e : e + 1, :]
            if kind == 0:
                gap_up[8 * s + source, u] = along_rows - along_lanes
            elif kind == 1:
                gap_down[8 * s + source, u] = along_rows - along_lanes
            else:
                plus = along_rows + along_lanes
                if source == s:
                    plus = plus - damping[s : s + 1, :]
                plus_down[8 * s + source, u] = plus

    def add_up(sums, src, block, k):
        u, q = place(k)
        for j in range(2):
            real, imag = src[2 * j], src[2 * j + 1]
            for s in range(2):
                gap = gap_up[8 * s + 2 * block + j, u, q : q + 8]
                sums[2 * s] = sums[2 * s] + gap * imag
                sums[2 * s + 1] = sums[2 * s + 1] - gap * real

    def add_down(sums, src, block, k):
        u, q = place(k)
        for j in range(2):
            real, imag = src[2 * j], src[2 * j + 1]
            for s in range(2):
                at = 8 * s + 2 * block + j
                gap, plus = gap_down[at, u, q : q + 8], plus_down[at, u, q : q + 8]
                sums[2 * s] = sums[2 * s] + gap * imag + plus * real
                sums[2 * s + 1] = sums[2 * s + 1] + plus * imag - gap * real

    def local(n):
        whole = [
            unpack([jnp.concatenate([own[n, PARTS * o + u, c] for o in range(3)], axis=0) for u in range(PARTS)])
            for c in range(4)
        ]
        right = jnp.dot(
            jnp.concatenate(whole, axis=0), ham_sq[...], precision=HIGHEST, preferred_element_type=jnp.float32
        )
        left = jnp.dot(
            ham_perm[:, :96], jnp.concatenate(whole, axis=1), precision=HIGHEST, preferred_element_type=jnp.float32
        )
        moved = [pack(left[:, 128 * c : 128 * (c + 1)] - right[96 * c : 96 * (c + 1)]) for c in range(4)]
        for k in range(SLABS):
            u, q = place(k)
            here = [part[u][q : q + 8] for part in moved]
            sums = [here[1], -here[0], here[3], -here[2]]
            add_down(sums, own.at[n, k], 0, k)
            for c in range(4):
                acc[k, c] = sums[c]

    def gather(n, p):
        arrive(n, LOWER_MODE + odd, p)
        relay(n, p)
        arrive(n, UPPER_MODE - odd, p)
        arrive(n, UPPER_TIER - odd, p)

        @pl.when(has_across)
        def _():
            arrive(n, LOWER_TIER + odd, p)

        for k in range(CUTS[p], CUTS[p + 1]):
            sums = [acc[k, c] for c in range(4)]
            add_down(sums, halo.at[n, LOWER_MODE, k], 2, k)
            add_up(sums, halo.at[n, UPPER_MODE, k], 2, k)
            add_down(sums, halo.at[n, LOWER_TIER, k], 1, k)
            add_up(sums, halo.at[n, UPPER_TIER, k], 1, k)
            for c in range(4):
                acc[k, c] = sums[c]

    def finish(n, p):
        arrive(n, UPPER_DIAG - odd, p)

        @pl.when(has_across)
        def _():
            arrive(n, LOWER_DIAG + odd, p)

        for k in range(CUTS[p], CUTS[p + 1]):
            u, q = place(k)
            sums = [acc[k, c] for c in range(4)]
            add_down(sums, halo.at[n, LOWER_DIAG, k], 3, k)
            add_up(sums, halo.at[n, UPPER_DIAG, k], 3, k)
            for c in range(4):
                term = (TIME_STEP / (n + 1)) * sums[c]
                if n < STAGES - 1:
                    own[n + 1, k, c] = term
                else:
                    total = term
                    for back in range(STAGES - 1, -1, -1):
                        total = total + own[back, k, c]
                    out_ref[c // 2, pl.ds(6 * q + 2 * u + c % 2, 8, stride=6), :] = total
        if n < STAGES - 1:
            send_own(n + 1, p)

    for n in range(STAGES):
        local(n)
        for p in range(PIECES + LAG):
            if p < PIECES:
                gather(n, p)
            if p >= LAG:
                finish(n, p - LAG)

    def sent(n, slot):
        pltpu.make_async_remote_copy(
            src_ref=own.at[n],
            dst_ref=halo.at[n, slot],
            send_sem=send_sem.at[n, slot],
            recv_sem=recv_sem.at[n, slot, 0],
            device_id=(partner, mode),
            device_id_type=MESH_ID,
        ).wait_send()

    for n in range(STAGES):
        sent(n, LOWER_MODE)
        sent(n, UPPER_MODE)
        sent(n, LOWER_TIER + odd)
        sent(n, LOWER_DIAG + odd)

        @pl.when(has_across)
        def _():
            sent(n, UPPER_TIER - odd)
            sent(n, UPPER_DIAG - odd)


def shards(ados, hamiltonian, couplings, rates, strength, occupancy, up_index, down_index):
    rows = ados.reshape(2, 2, 72, 128).transpose(0, 2, 1, 3).reshape(2, 144, 128)
    operands = (
        rows, hamiltonian, couplings, rates.reshape(1, -1), strength,
        occupancy.reshape(2, -1), up_index.reshape(2, -1), down_index.reshape(2, -1),
    )
    real = jnp.float32
    operands = [pltpu.with_memory_space_constraint(x, pltpu.HBM) for x in operands]
    done = pl.pallas_call(
        kernel,
        out_shape=jax.ShapeDtypeStruct((2, 144, 128), real),
        in_specs=[pl.BlockSpec(memory_space=pltpu.HBM)] * 8,
        out_specs=pl.BlockSpec(memory_space=pltpu.VMEM),
        scratch_shapes=[pltpu.VMEM(x.shape, x.dtype) for x in operands] + [
            pltpu.SemaphoreType.DMA((8,)),
            pltpu.VMEM((STAGES, SLABS, 4, 8, 128), real),
            pltpu.VMEM((STAGES, 6, SLABS, 4, 8, 128), real),
            pltpu.VMEM((SLABS, 4, 8, 128), real),
            pltpu.VMEM((16, PARTS, GROUPS, 128), real),
            pltpu.VMEM((16, PARTS, GROUPS, 128), real),
            pltpu.VMEM((16, PARTS, GROUPS, 128), real),
            pltpu.VMEM((128, 128), real),
            pltpu.VMEM((96, 128), real),
            pltpu.VMEM((128, 128), real),
            pltpu.SemaphoreType.DMA((STAGES, 6)),
            pltpu.SemaphoreType.DMA((STAGES, 6, PIECES)),
        ],
        compiler_params=pltpu.CompilerParams(collective_id=0, has_side_effects=True, vmem_limit_bytes=16 * 2**20),
    )(*operands)
    return done.reshape(2, 72, 2, 128).transpose(0, 2, 1, 3).reshape(ados.shape)


def solution(mesh):
    split = P("tier", "mode", None, None)
    in_specs = (P("tier", "mode", None, None, None), P(), P(), P(), P(), split, split, split)
    out_specs = P("tier", "mode", None, None, None)
    return jax.shard_map(shards, mesh=mesh, in_specs=in_specs, out_specs=out_specs, check_vma=False)
```

```python
import jax
import jax.numpy as jnp
from jax import lax
from jax.experimental import pallas as pl
from jax.experimental.pallas import tpu as pltpu
from jax.sharding import PartitionSpec as P

TIME_STEP = 0.3
STAGES = 4
HIGHEST = lax.Precision.HIGHEST
MESH_ID = pl.DeviceIdType.MESH

LOWER_TIER, UPPER_TIER, LOWER_MODE, UPPER_MODE, LOWER_DIAG, UPPER_DIAG = range(6)
PARTS = 3
SLABS = 9
GROUPS = 24
CUTS = (0, 1, 3, 5, 7, 9)
PIECES = len(CUTS) - 1


def lane_index():
    return lax.broadcasted_iota(jnp.int32, (GROUPS, 128), 1)


def widen(row):
    lane = lax.broadcasted_iota(jnp.int32, row.shape, 1)
    by96, by64, by32 = (pltpu.roll(row, shift, 1) for shift in (96, 64, 32))
    return (
        jnp.where(lane < 96, row, by96),
        jnp.where(lane < 64, by96, by64),
        jnp.where(lane < 32, by64, by32),
    )


def unpack(parts):
    lane = lane_index()
    first, second, third = parts
    return jnp.concatenate(
        [
            first,
            jnp.where(lane < 32, pltpu.roll(first, 32, 1), pltpu.roll(second, 32, 1)),
            jnp.where(lane < 64, pltpu.roll(second, 64, 1), pltpu.roll(third, 64, 1)),
            pltpu.roll(third, 96, 1),
        ],
        axis=0,
    )


def pack(rows):
    lane = lane_index()
    part = [rows[GROUPS * p : GROUPS * (p + 1)] for p in range(4)]
    one96, two64 = pltpu.roll(part[1], 96, 1), pltpu.roll(part[2], 64, 1)
    return (
        jnp.where(lane < 96, part[0], one96),
        jnp.where(lane < 64, one96, two64),
        jnp.where(lane < 32, two64, pltpu.roll(part[3], 32, 1)),
    )


def kernel(
    a_hbm, ham_hbm, cpl_hbm, rates_hbm, strength_hbm, occ_hbm, up_hbm, down_hbm,
    out_ref,
    a_ref, ham_ref, cpl_ref, rates_ref, strength_ref, occ_ref, up_ref, down_ref, load_sem,
    own, halo, acc, gap_up, gap_down, plus_down, ham_sq, ham_perm, tall, send_sem, recv_sem,
):
    tier, mode = lax.axis_index("tier"), lax.axis_index("mode")
    tiers, modes = lax.axis_size("tier"), lax.axis_size("mode")
    next_mode, prev_mode = lax.rem(mode + 1, modes), lax.rem(mode + modes - 1, modes)
    odd = lax.rem(tier, 2)
    partner = tier + 1 - 2 * odd
    near_mode = lax.rem(mode + modes + 1 - 2 * odd, modes)
    across = lax.rem(tier + 2 * odd + tiers - 1, tiers)
    across_mode = lax.rem(mode + 2 * odd + modes - 1, modes)
    has_across = jnp.logical_and(tier > 0, tier < tiers - 1)

    barrier = pltpu.get_barrier_semaphore()

    def greet(device):
        pl.semaphore_signal(barrier, inc=1, device_id=device, device_id_type=MESH_ID)

    greet((tier, next_mode))
    greet((tier, prev_mode))
    greet((partner, mode))

    @pl.when(has_across)
    def _():
        greet((across, mode))
        greet((across, across_mode))

    loads = [
        pltpu.make_async_copy(src, dst, load_sem.at[i])
        for i, (src, dst) in enumerate(
            zip(
                (a_hbm, ham_hbm, cpl_hbm, rates_hbm, strength_hbm, occ_hbm, up_hbm, down_hbm),
                (a_ref, ham_ref, cpl_ref, rates_ref, strength_ref, occ_ref, up_ref, down_ref),
            )
        )
    ]
    for load in loads:
        load.start()
    loads[0].wait()

    def place(k):
        return k % PARTS, 8 * (k // PARTS)

    for k in range(SLABS):
        u, q = place(k)
        for c in range(4):
            own[0, k, c] = a_ref[c // 2, pl.ds(6 * q + 2 * u + c % 2, 8, stride=6), :]

    @pl.when(has_across)
    def _():
        pl.semaphore_wait(barrier, 5)

    @pl.when(jnp.logical_not(has_across))
    def _():
        pl.semaphore_wait(barrier, 3)

    def copy(n, slot, p, src, device):
        span = pl.ds(CUTS[p], CUTS[p + 1] - CUTS[p])
        return pltpu.make_async_remote_copy(
            src_ref=src.at[span],
            dst_ref=halo.at[n, slot, span],
            send_sem=send_sem.at[n, slot],
            recv_sem=recv_sem.at[n, slot, p],
            device_id=device,
            device_id_type=MESH_ID,
        )

    def arrive(n, slot, p):
        copy(n, slot, p, own.at[n], (partner, mode)).wait_recv()

    def send_own(n, p):
        mine = own.at[n]
        copy(n, LOWER_MODE + odd, p, mine, (tier, near_mode)).start()

        @pl.when(has_across)
        def _():
            copy(n, UPPER_DIAG - odd, p, mine, (across, across_mode)).start()

        copy(n, UPPER_MODE - odd, p, mine, (tier, across_mode)).start()

        @pl.when(has_across)
        def _():
            copy(n, UPPER_TIER - odd, p, mine, (across, mode)).start()

        copy(n, LOWER_TIER + odd, p, mine, (partner, mode)).start()

    def relay(n, p):
        copy(n, LOWER_DIAG + odd, p, halo.at[n, LOWER_MODE + odd], (partner, mode)).start()

    for p in range(PIECES):
        send_own(0, p)

    blank = jnp.zeros((4, 8, 128), jnp.float32)

    @pl.when(jnp.logical_not(has_across))
    def _():
        for n in range(STAGES):
            for k in range(SLABS):
                halo[n, LOWER_TIER + odd, k] = blank
                halo[n, LOWER_DIAG + odd, k] = blank

    for load in loads[1:]:
        load.wait()

    raw = ham_ref[...]
    ham_sq[...] = jnp.zeros((128, 128), jnp.float32)
    ham_sq[:96, :96] = 0.5 * (raw + raw.T)
    rows = jnp.concatenate([ham_sq[pl.ds(p, GROUPS, stride=4), :] for p in range(4)], axis=0)
    tall[...] = jnp.concatenate([rows, jnp.zeros((32, 128), jnp.float32)], axis=0).T
    ham_perm[...] = jnp.concatenate([tall[pl.ds(p, GROUPS, stride=4), :] for p in range(4)], axis=0)

    level = occ_ref[...].astype(jnp.float32)
    named = lax.broadcasted_iota(jnp.int32, (8, 16), 0)
    ups, down_re, down_im = [], [], []
    for s in range(2):
        up_mask = (up_ref[s : s + 1, :] == named).astype(jnp.float32)
        down_mask = (down_ref[s : s + 1, :] == named).astype(jnp.float32) * level[s : s + 1, :]
        ups.append(up_mask)
        down_re.append(down_mask * strength_ref[0:1, :])
        down_im.append(down_mask * strength_ref[1:2, :])
    own_rows = lax.broadcasted_iota(jnp.int32, (8, 16), 0) < 2
    down_re = [d + jnp.where(own_rows, v, 0.0) for d, v in zip(down_re, ups)]
    mix = jnp.concatenate(ups + down_re + down_im, axis=0)
    cpl = cpl_ref[...]
    wide_cpl = jnp.concatenate([cpl, jnp.zeros((16, 32), jnp.float32)], axis=1)
    by_lane = jnp.dot(mix, wide_cpl, precision=HIGHEST, preferred_element_type=jnp.float32)
    flat = lax.dot_general(
        wide_cpl, mix, (((0,), (1,)), ((), ())), precision=HIGHEST, preferred_element_type=jnp.float32
    )
    tall[:, :48] = flat
    columns = [tall[pl.ds(p, GROUPS, stride=4), :] for p in range(4)]
    lane = lane_index()
    lanes_wide = widen(by_lane)
    damping = jnp.sum(level * rates_ref[...], axis=1, keepdims=True)
    for e in range(48):
        kind, s, source = e // 16, e // 8 % 2, e % 8
        if kind == 0 and source < 2:
            continue
        spread = [jnp.broadcast_to(columns[p][:, e : e + 1], (GROUPS, 128)) for p in range(4)]
        for u in range(PARTS):
            along_rows = jnp.where(lane < (96, 64, 32)[u], spread[u], spread[u + 1])
            along_lanes = lanes_wide[u][e : e + 1, :]
            if kind == 0:
                gap_up[8 * s + source, u] = along_rows - along_lanes
            elif kind == 1:
                gap_down[8 * s + source, u] = along_rows - along_lanes
            else:
                plus = along_rows + along_lanes
                if source == s:
                    plus = plus - damping[s : s + 1, :]
                plus_down[8 * s + source, u] = plus

    def add_up(sums, src, block, k):
        u, q = place(k)
        for j in range(2):
            real, imag = src[2 * j], src[2 * j + 1]
            for s in range(2):
                gap = gap_up[8 * s + 2 * block + j, u, q : q + 8]
                sums[2 * s] = sums[2 * s] + gap * imag
                sums[2 * s + 1] = sums[2 * s + 1] - gap * real

    def add_down(sums, src, block, k):
        u, q = place(k)
        for j in range(2):
            real, imag = src[2 * j], src[2 * j + 1]
            for s in range(2):
                at = 8 * s + 2 * block + j
                gap, plus = gap_down[at, u, q : q + 8], plus_down[at, u, q : q + 8]
                sums[2 * s] = sums[2 * s] + gap * imag + plus * real
                sums[2 * s + 1] = sums[2 * s + 1] + plus * imag - gap * real

    def local(n):
        whole = [
            unpack([jnp.concatenate([own[n, PARTS * o + u, c] for o in range(3)], axis=0) for u in range(PARTS)])
            for c in range(4)
        ]
        right = jnp.dot(
            jnp.concatenate(whole, axis=0), ham_sq[...], precision=HIGHEST, preferred_element_type=jnp.float32
        )
        left = jnp.dot(
            ham_perm[:, :96], jnp.concatenate(whole, axis=1), precision=HIGHEST, preferred_element_type=jnp.float32
        )
        moved = [pack(left[:, 128 * c : 128 * (c + 1)] - right[96 * c : 96 * (c + 1)]) for c in range(4)]
        for k in range(SLABS):
            u, q = place(k)
            here = [part[u][q : q + 8] for part in moved]
            sums = [here[1], -here[0], here[3], -here[2]]
            add_down(sums, own.at[n, k], 0, k)
            for c in range(4):
                acc[k, c] = sums[c]

    def pass_on(n, p):
        arrive(n, LOWER_MODE + odd, p)
        relay(n, p)

    def gather(n, p):
        arrive(n, UPPER_MODE - odd, p)
        arrive(n, UPPER_TIER - odd, p)

        @pl.when(has_across)
        def _():
            arrive(n, LOWER_TIER + odd, p)

        for k in range(CUTS[p], CUTS[p + 1]):
            sums = [acc[k, c] for c in range(4)]
            add_down(sums, halo.at[n, LOWER_MODE, k], 2, k)
            add_up(sums, halo.at[n, UPPER_MODE, k], 2, k)
            add_down(sums, halo.at[n, LOWER_TIER, k], 1, k)
            add_up(sums, halo.at[n, UPPER_TIER, k], 1, k)
            for c in range(4):
                acc[k, c] = sums[c]

    def finish(n, p):
        arrive(n, UPPER_DIAG - odd, p)

        @pl.when(has_across)
        def _():
            arrive(n, LOWER_DIAG + odd, p)

        for k in range(CUTS[p], CUTS[p + 1]):
            u, q = place(k)
            sums = [acc[k, c] for c in range(4)]
            add_down(sums, halo.at[n, LOWER_DIAG, k], 3, k)
            add_up(sums, halo.at[n, UPPER_DIAG, k], 3, k)
            for c in range(4):
                term = (TIME_STEP / (n + 1)) * sums[c]
                if n < STAGES - 1:
                    own[n + 1, k, c] = term
                else:
                    total = term
                    for back in range(STAGES - 1, -1, -1):
                        total = total + own[back, k, c]
                    out_ref[c // 2, pl.ds(6 * q + 2 * u + c % 2, 8, stride=6), :] = total
        if n < STAGES - 1:
            send_own(n + 1, p)

    for n in range(STAGES):
        local(n)
        pass_on(n, 0)
        for p in range(PIECES):
            gather(n, p)
            if p + 1 < PIECES:
                pass_on(n, p + 1)
            finish(n, p)

    def sent(n, slot):
        pltpu.make_async_remote_copy(
            src_ref=own.at[n],
            dst_ref=halo.at[n, slot],
            send_sem=send_sem.at[n, slot],
            recv_sem=recv_sem.at[n, slot, 0],
            device_id=(partner, mode),
            device_id_type=MESH_ID,
        ).wait_send()

    for n in range(STAGES):
        sent(n, LOWER_MODE)
        sent(n, UPPER_MODE)
        sent(n, LOWER_TIER + odd)
        sent(n, LOWER_DIAG + odd)

        @pl.when(has_across)
        def _():
            sent(n, UPPER_TIER - odd)
            sent(n, UPPER_DIAG - odd)


def shards(ados, hamiltonian, couplings, rates, strength, occupancy, up_index, down_index):
    rows = ados.reshape(2, 2, 72, 128).transpose(0, 2, 1, 3).reshape(2, 144, 128)
    operands = (
        rows, hamiltonian, couplings, rates.reshape(1, -1), strength,
        occupancy.reshape(2, -1), up_index.reshape(2, -1), down_index.reshape(2, -1),
    )
    real = jnp.float32
    operands = [pltpu.with_memory_space_constraint(x, pltpu.HBM) for x in operands]
    done = pl.pallas_call(
        kernel,
        out_shape=jax.ShapeDtypeStruct((2, 144, 128), real),
        in_specs=[pl.BlockSpec(memory_space=pltpu.HBM)] * 8,
        out_specs=pl.BlockSpec(memory_space=pltpu.VMEM),
        scratch_shapes=[pltpu.VMEM(x.shape, x.dtype) for x in operands] + [
            pltpu.SemaphoreType.DMA((8,)),
            pltpu.VMEM((STAGES, SLABS, 4, 8, 128), real),
            pltpu.VMEM((STAGES, 6, SLABS, 4, 8, 128), real),
            pltpu.VMEM((SLABS, 4, 8, 128), real),
            pltpu.VMEM((16, PARTS, GROUPS, 128), real),
            pltpu.VMEM((16, PARTS, GROUPS, 128), real),
            pltpu.VMEM((16, PARTS, GROUPS, 128), real),
            pltpu.VMEM((128, 128), real),
            pltpu.VMEM((96, 128), real),
            pltpu.VMEM((128, 128), real),
            pltpu.SemaphoreType.DMA((STAGES, 6)),
            pltpu.SemaphoreType.DMA((STAGES, 6, PIECES)),
        ],
        compiler_params=pltpu.CompilerParams(collective_id=0, has_side_effects=True, vmem_limit_bytes=16 * 2**20),
    )(*operands)
    return done.reshape(2, 72, 2, 128).transpose(0, 2, 1, 3).reshape(ados.shape)


def solution(mesh):
    split = P("tier", "mode", None, None)
    in_specs = (P("tier", "mode", None, None, None), P(), P(), P(), P(), split, split, split)
    out_specs = P("tier", "mode", None, None, None)
    return jax.shard_map(shards, mesh=mesh, in_specs=in_specs, out_specs=out_specs, check_vma=False)
```

```python
import jax
import jax.numpy as jnp
from jax import lax
from jax.experimental import pallas as pl
from jax.experimental.pallas import tpu as pltpu
from jax.sharding import PartitionSpec as P

TIME_STEP = 0.3
STAGES = 4
HIGHEST = lax.Precision.HIGHEST
MESH_ID = pl.DeviceIdType.MESH

LOWER_TIER, UPPER_TIER, LOWER_MODE, UPPER_MODE, LOWER_DIAG, UPPER_DIAG = range(6)
PARTS = 3
SLABS = 9
GROUPS = 24
CUTS = (0, 1, 3, 5, 7, 9)
PIECES = len(CUTS) - 1


def lane_index():
    return lax.broadcasted_iota(jnp.int32, (GROUPS, 128), 1)


def widen(row):
    lane = lax.broadcasted_iota(jnp.int32, row.shape, 1)
    by96, by64, by32 = (pltpu.roll(row, shift, 1) for shift in (96, 64, 32))
    return (
        jnp.where(lane < 96, row, by96),
        jnp.where(lane < 64, by96, by64),
        jnp.where(lane < 32, by64, by32),
    )


def unpack(parts):
    lane = lane_index()
    first, second, third = parts
    return jnp.concatenate(
        [
            first,
            jnp.where(lane < 32, pltpu.roll(first, 32, 1), pltpu.roll(second, 32, 1)),
            jnp.where(lane < 64, pltpu.roll(second, 64, 1), pltpu.roll(third, 64, 1)),
            pltpu.roll(third, 96, 1),
        ],
        axis=0,
    )


def pack(rows):
    lane = lane_index()
    part = [rows[GROUPS * p : GROUPS * (p + 1)] for p in range(4)]
    one96, two64 = pltpu.roll(part[1], 96, 1), pltpu.roll(part[2], 64, 1)
    return (
        jnp.where(lane < 96, part[0], one96),
        jnp.where(lane < 64, one96, two64),
        jnp.where(lane < 32, two64, pltpu.roll(part[3], 32, 1)),
    )


def kernel(
    a_hbm, ham_hbm, cpl_hbm, rates_hbm, strength_hbm, occ_hbm, up_hbm, down_hbm,
    out_ref,
    a_ref, ham_ref, cpl_ref, rates_ref, strength_ref, occ_ref, up_ref, down_ref, load_sem,
    own, halo, acc, gap_up, gap_down, plus_down, ham_sq, ham_perm, tall, send_sem, recv_sem,
):
    tier, mode = lax.axis_index("tier"), lax.axis_index("mode")
    tiers, modes = lax.axis_size("tier"), lax.axis_size("mode")
    next_mode, prev_mode = lax.rem(mode + 1, modes), lax.rem(mode + modes - 1, modes)
    odd = lax.rem(tier, 2)
    partner = tier + 1 - 2 * odd
    near_mode = lax.rem(mode + modes + 1 - 2 * odd, modes)
    across = lax.rem(tier + 2 * odd + tiers - 1, tiers)
    across_mode = lax.rem(mode + 2 * odd + modes - 1, modes)
    has_across = jnp.logical_and(tier > 0, tier < tiers - 1)

    barrier = pltpu.get_barrier_semaphore()

    def greet(device):
        pl.semaphore_signal(barrier, inc=1, device_id=device, device_id_type=MESH_ID)

    greet((tier, next_mode))
    greet((tier, prev_mode))
    greet((partner, mode))

    @pl.when(has_across)
    def _():
        greet((across, mode))
        greet((across, across_mode))

    loads = [
        pltpu.make_async_copy(src, dst, load_sem.at[i])
        for i, (src, dst) in enumerate(
            zip(
                (a_hbm, ham_hbm, cpl_hbm, rates_hbm, strength_hbm, occ_hbm, up_hbm, down_hbm),
                (a_ref, ham_ref, cpl_ref, rates_ref, strength_ref, occ_ref, up_ref, down_ref),
            )
        )
    ]
    for load in loads:
        load.start()
    loads[0].wait()

    def place(k):
        return k % PARTS, 8 * (k // PARTS)

    for k in range(SLABS):
        u, q = place(k)
        for c in range(4):
            own[0, k, c] = a_ref[c // 2, pl.ds(6 * q + 2 * u + c % 2, 8, stride=6), :]

    @pl.when(has_across)
    def _():
        pl.semaphore_wait(barrier, 5)

    @pl.when(jnp.logical_not(has_across))
    def _():
        pl.semaphore_wait(barrier, 3)

    def copy(n, slot, p, src, device):
        span = pl.ds(CUTS[p], CUTS[p + 1] - CUTS[p])
        return pltpu.make_async_remote_copy(
            src_ref=src.at[span],
            dst_ref=halo.at[n, slot, span],
            send_sem=send_sem.at[n, slot],
            recv_sem=recv_sem.at[n, slot, p],
            device_id=device,
            device_id_type=MESH_ID,
        )

    def arrive(n, slot, p):
        copy(n, slot, p, own.at[n], (partner, mode)).wait_recv()

    def send_own(n, p):
        mine = own.at[n]
        copy(n, LOWER_MODE + odd, p, mine, (tier, near_mode)).start()

        @pl.when(has_across)
        def _():
            copy(n, UPPER_DIAG - odd, p, mine, (across, across_mode)).start()
            copy(n, UPPER_TIER - odd, p, mine, (across, mode)).start()

        copy(n, UPPER_MODE - odd, p, mine, (tier, across_mode)).start()

        copy(n, LOWER_TIER + odd, p, mine, (partner, mode)).start()

    def relay(n, p):
        copy(n, LOWER_DIAG + odd, p, halo.at[n, LOWER_MODE + odd], (partner, mode)).start()

    for p in range(PIECES):
        send_own(0, p)

    blank = jnp.zeros((4, 8, 128), jnp.float32)

    @pl.when(jnp.logical_not(has_across))
    def _():
        for n in range(STAGES):
            for k in range(SLABS):
                halo[n, LOWER_TIER + odd, k] = blank
                halo[n, LOWER_DIAG + odd, k] = blank

    for load in loads[1:]:
        load.wait()

    raw = ham_ref[...]
    ham_sq[...] = jnp.zeros((128, 128), jnp.float32)
    ham_sq[:96, :96] = 0.5 * (raw + raw.T)
    rows = jnp.concatenate([ham_sq[pl.ds(p, GROUPS, stride=4), :] for p in range(4)], axis=0)
    tall[...] = jnp.concatenate([rows, jnp.zeros((32, 128), jnp.float32)], axis=0).T
    ham_perm[...] = jnp.concatenate([tall[pl.ds(p, GROUPS, stride=4), :] for p in range(4)], axis=0)

    level = occ_ref[...].astype(jnp.float32)
    named = lax.broadcasted_iota(jnp.int32, (8, 16), 0)
    ups, down_re, down_im = [], [], []
    for s in range(2):
        up_mask = (up_ref[s : s + 1, :] == named).astype(jnp.float32)
        down_mask = (down_ref[s : s + 1, :] == named).astype(jnp.float32) * level[s : s + 1, :]
        ups.append(up_mask)
        down_re.append(down_mask * strength_ref[0:1, :])
        down_im.append(down_mask * strength_ref[1:2, :])
    own_rows = lax.broadcasted_iota(jnp.int32, (8, 16), 0) < 2
    down_re = [d + jnp.where(own_rows, v, 0.0) for d, v in zip(down_re, ups)]
    mix = jnp.concatenate(ups + down_re + down_im, axis=0)
    cpl = cpl_ref[...]
    wide_cpl = jnp.concatenate([cpl, jnp.zeros((16, 32), jnp.float32)], axis=1)
    by_lane = jnp.dot(mix, wide_cpl, precision=HIGHEST, preferred_element_type=jnp.float32)
    flat = lax.dot_general(
        wide_cpl, mix, (((0,), (1,)), ((), ())), precision=HIGHEST, preferred_element_type=jnp.float32
    )
    tall[:, :48] = flat
    columns = [tall[pl.ds(p, GROUPS, stride=4), :] for p in range(4)]
    lane = lane_index()
    lanes_wide = widen(by_lane)
    damping = jnp.sum(level * rates_ref[...], axis=1, keepdims=True)
    for e in range(48):
        kind, s, source = e // 16, e // 8 % 2, e % 8
        if kind == 0 and source < 2:
            continue
        spread = [jnp.broadcast_to(columns[p][:, e : e + 1], (GROUPS, 128)) for p in range(4)]
        for u in range(PARTS):
            along_rows = jnp.where(lane < (96, 64, 32)[u], spread[u], spread[u + 1])
            along_lanes = lanes_wide[u][e : e + 1, :]
            if kind == 0:
                gap_up[8 * s + source, u] = along_rows - along_lanes
            elif kind == 1:
                gap_down[8 * s + source, u] = along_rows - along_lanes
            else:
                plus = along_rows + along_lanes
                if source == s:
                    plus = plus - damping[s : s + 1, :]
                plus_down[8 * s + source, u] = plus

    def add_up(sums, src, block, k):
        u, q = place(k)
        for j in range(2):
            real, imag = src[2 * j], src[2 * j + 1]
            for s in range(2):
                gap = gap_up[8 * s + 2 * block + j, u, q : q + 8]
                sums[2 * s] = sums[2 * s] + gap * imag
                sums[2 * s + 1] = sums[2 * s + 1] - gap * real

    def add_down(sums, src, block, k):
        u, q = place(k)
        for j in range(2):
            real, imag = src[2 * j], src[2 * j + 1]
            for s in range(2):
                at = 8 * s + 2 * block + j
                gap, plus = gap_down[at, u, q : q + 8], plus_down[at, u, q : q + 8]
                sums[2 * s] = sums[2 * s] + gap * imag + plus * real
                sums[2 * s + 1] = sums[2 * s + 1] + plus * imag - gap * real

    def local(n):
        whole = [
            unpack([jnp.concatenate([own[n, PARTS * o + u, c] for o in range(3)], axis=0) for u in range(PARTS)])
            for c in range(4)
        ]
        right = jnp.dot(
            jnp.concatenate(whole, axis=0), ham_sq[...], precision=HIGHEST, preferred_element_type=jnp.float32
        )
        left = jnp.dot(
            ham_perm[:, :96], jnp.concatenate(whole, axis=1), precision=HIGHEST, preferred_element_type=jnp.float32
        )
        moved = [pack(left[:, 128 * c : 128 * (c + 1)] - right[96 * c : 96 * (c + 1)]) for c in range(4)]
        for k in range(SLABS):
            u, q = place(k)
            here = [part[u][q : q + 8] for part in moved]
            sums = [here[1], -here[0], here[3], -here[2]]
            add_down(sums, own.at[n, k], 0, k)
            for c in range(4):
                acc[k, c] = sums[c]

    def pass_on(n, p):
        arrive(n, LOWER_MODE + odd, p)
        relay(n, p)

    def gather(n, p):
        arrive(n, UPPER_MODE - odd, p)
        arrive(n, UPPER_TIER - odd, p)

        @pl.when(has_across)
        def _():
            arrive(n, LOWER_TIER + odd, p)

        for k in range(CUTS[p], CUTS[p + 1]):
            sums = [acc[k, c] for c in range(4)]
            add_down(sums, halo.at[n, LOWER_MODE, k], 2, k)
            add_up(sums, halo.at[n, UPPER_MODE, k], 2, k)
            add_down(sums, halo.at[n, LOWER_TIER, k], 1, k)
            add_up(sums, halo.at[n, UPPER_TIER, k], 1, k)
            for c in range(4):
                acc[k, c] = sums[c]

    def finish(n, p):
        arrive(n, UPPER_DIAG - odd, p)

        @pl.when(has_across)
        def _():
            arrive(n, LOWER_DIAG + odd, p)

        for k in range(CUTS[p], CUTS[p + 1]):
            u, q = place(k)
            sums = [acc[k, c] for c in range(4)]
            add_down(sums, halo.at[n, LOWER_DIAG, k], 3, k)
            add_up(sums, halo.at[n, UPPER_DIAG, k], 3, k)
            for c in range(4):
                term = (TIME_STEP / (n + 1)) * sums[c]
                if n < STAGES - 1:
                    own[n + 1, k, c] = term
                else:
                    total = term
                    for back in range(STAGES - 1, -1, -1):
                        total = total + own[back, k, c]
                    out_ref[c // 2, pl.ds(6 * q + 2 * u + c % 2, 8, stride=6), :] = total
        if n < STAGES - 1:
            send_own(n + 1, p)

    def sent(n, slot):
        pltpu.make_async_remote_copy(
            src_ref=own.at[n],
            dst_ref=halo.at[n, slot],
            send_sem=send_sem.at[n, slot],
            recv_sem=recv_sem.at[n, slot, 0],
            device_id=(partner, mode),
            device_id_type=MESH_ID,
        ).wait_send()

    def all_sent(n):
        sent(n, LOWER_MODE)
        sent(n, UPPER_MODE)
        sent(n, LOWER_TIER + odd)
        sent(n, LOWER_DIAG + odd)

        @pl.when(has_across)
        def _():
            sent(n, UPPER_TIER - odd)
            sent(n, UPPER_DIAG - odd)

    for n in range(STAGES):
        local(n)
        pass_on(n, 0)
        for p in range(PIECES):
            gather(n, p)
            if p + 1 < PIECES:
                pass_on(n, p + 1)
            finish(n, p)
            if p == PIECES - 2 and n > 0:
                all_sent(n - 1)

    all_sent(STAGES - 1)


def shards(ados, hamiltonian, couplings, rates, strength, occupancy, up_index, down_index):
    rows = ados.reshape(2, 2, 72, 128).transpose(0, 2, 1, 3).reshape(2, 144, 128)
    operands = (
        rows, hamiltonian, couplings, rates.reshape(1, -1), strength,
        occupancy.reshape(2, -1), up_index.reshape(2, -1), down_index.reshape(2, -1),
    )
    real = jnp.float32
    operands = [pltpu.with_memory_space_constraint(x, pltpu.HBM) for x in operands]
    done = pl.pallas_call(
        kernel,
        out_shape=jax.ShapeDtypeStruct((2, 144, 128), real),
        in_specs=[pl.BlockSpec(memory_space=pltpu.HBM)] * 8,
        out_specs=pl.BlockSpec(memory_space=pltpu.VMEM),
        scratch_shapes=[pltpu.VMEM(x.shape, x.dtype) for x in operands] + [
            pltpu.SemaphoreType.DMA((8,)),
            pltpu.VMEM((STAGES, SLABS, 4, 8, 128), real),
            pltpu.VMEM((STAGES, 6, SLABS, 4, 8, 128), real),
            pltpu.VMEM((SLABS, 4, 8, 128), real),
            pltpu.VMEM((16, PARTS, GROUPS, 128), real),
            pltpu.VMEM((16, PARTS, GROUPS, 128), real),
            pltpu.VMEM((16, PARTS, GROUPS, 128), real),
            pltpu.VMEM((128, 128), real),
            pltpu.VMEM((96, 128), real),
            pltpu.VMEM((128, 128), real),
            pltpu.SemaphoreType.DMA((STAGES, 6)),
            pltpu.SemaphoreType.DMA((STAGES, 6, PIECES)),
        ],
        compiler_params=pltpu.CompilerParams(collective_id=0, has_side_effects=True, vmem_limit_bytes=16 * 2**20),
    )(*operands)
    return done.reshape(2, 72, 2, 128).transpose(0, 2, 1, 3).reshape(ados.shape)


def solution(mesh):
    split = P("tier", "mode", None, None)
    in_specs = (P("tier", "mode", None, None, None), P(), P(), P(), P(), split, split, split)
    out_specs = P("tier", "mode", None, None, None)
    return jax.shard_map(shards, mesh=mesh, in_specs=in_specs, out_specs=out_specs, check_vma=False)
```
